32 devices in a mesh: groups: 2 (over x), blk: 4 (over y, core), rows: 4 (over z).
Axes of the slice: x: 2, y: 2, z: 4, core: 2. Of those that a mesh axis runs over, the one named last changes fastest.
Arguments:
- tiles: float32 [64, 4, 4, 256, 256], P(('groups', 'rows'), 'blk'), parts along dimension 0, may hold values from 0 to 0.00078125
- tile_index: int32 [64, 4, 4], P(('groups', 'rows'), 'blk'), parts along dimension 0, may hold values from 0 to 7
- tiles_in_use: int32 [64, 4], P(('groups', 'rows'), 'blk'), parts along dimension 0, may hold values from 1 to 4, 10 in all within a row
- demand: int32 [128], P('groups'), parts along dimension 0, may hold values from 0 to 63, each once
- profiles: float32 [128, 8192], P('groups', 'blk'), parts along dimension 0, may hold values from 0.05 to 2.7, as said below
- capacity: float32 [128, 8192], P('groups', 'rows'), parts along dimension 0, may hold values from 0.05 to 4.5, as said below
- start_rates: float32 [128, 8192], P('groups', 'blk'), parts along dimension 0, may hold values from 0 to 1
- start_duals: float32 [128, 8192], P('groups', 'rows'), parts along dimension 0, may hold values from 0 to 1
- primal_weight: float32 [128], P('groups'), parts along dimension 0, may hold values from 0.5 to 2
Outputs:
- rates: float32 [128, 8192], P('groups', 'blk'), parts along dimension 0
- duals: float32 [128, 8192], P('groups', 'rows'), parts along dimension 0
- weight: float32 [128], P('groups'), parts along dimension 0
The draws below stay inside these ranges and needn't reach their ends.
There are 2 independent parts, one for each index of `groups`. The reference program is written for one: setup_inputs(seed, part) draws one part's arguments, and reference() takes and returns one part's arrays. A program takes and returns all parts, laid end to end along the dimension named above; each array names one. Nothing has to cross between parts.
Inputs may be any that keep to these rules, and one draw needn't show every extreme that they name: `tile_index`: each slot names a link block inside its own column shard. `tiles_in_use`: for every row block the counts over the 4 column shards add up to 10, and the largest of them is 4. `demand`: each scenario names a different profile. `profiles`: positive weights. `capacity`: positive capacities.
All inputs are finite; a program needn't handle non-finite values.
Results may differ from the reference program's by a relative error of at most 0.00011.
Values sent between devices are 32-bit elements; how exact they have to be, the bound alone decides.
A program may use at most 64 MiB of HBM per device.

```python
import math
import jax
import jax.numpy as jnp
import numpy as np
from jax import lax

TILE = 256
SCEN = 64
SLOTS_PER_BLOCK = 4
ITERS = 3
CBB = 8
CONS_BLOCKS = 32
CONS = 8192
LINK_BLOCKS = 32
LINKS = 8192
LIVE_ROW = 10
N_BLK = 4


def draw_profiles(key, part):
    position = jnp.arange(LINKS, dtype=jnp.float32) / LINKS
    base = jnp.exp(jax.random.uniform(key, (SCEN, LINKS), jnp.float32, math.log(0.05), math.log(0.3)))
    ramp = jnp.exp(math.log(3.0) * position)
    return base * ramp[None, :]


def draw_capacity(key, part):
    position = jnp.arange(CONS, dtype=jnp.float32) / CONS
    base = jax.random.uniform(key, (SCEN, CONS), jnp.float32, 0.15, 0.45)
    ramp = jnp.exp(math.log(3.0) * position)
    return base * ramp[None, :]


def with_ends(entries, key, low, high):
    spot = [jax.random.randint(jax.random.fold_in(key, axis), (), 0, length) for axis, length in enumerate(entries.shape)]
    longest = entries.shape.index(max(entries.shape))
    neighbour = spot[:longest] + [(spot[longest] + 1) % entries.shape[longest]] + spot[longest + 1:]
    return entries.at[tuple(spot)].set(low).at[tuple(neighbour)].set(high)


def level_of(rng, extent, split, smallest, high):
    def one(dim, shards_of):
        steps = jax.random.uniform(jax.random.fold_in(jax.random.fold_in(rng, 6), dim), (shards_of,), jnp.float32, smallest / len(split), high / len(split))
        return jnp.repeat(jnp.exp(steps), extent[dim] // shards_of).reshape((-1,) + (1,) * (len(extent) - dim - 1))

    loudness = one(*split[0])
    for cut in split[1:]:
        loudness = loudness * one(*cut)
    return loudness


def length_profile(amount, total, reach, lean):
    loads = [(1 << 20) // math.isqrt(grade ** lean) + 1 for grade in range(2, amount + 1)]
    spare, counts = total - reach - (amount - 1), [1] * (amount - 1)
    while spare > 0:
        movable = [i for i in range(amount - 1) if counts[i] < reach]
        pool, remaining = sum([loads[i] for i in movable]), spare
        for i in movable:
            addition = min(reach - counts[i], max(1, remaining * loads[i] // pool), spare)
            counts[i] = counts[i] + addition
            spare = spare - addition
    return np.array([reach] + counts)


def ragged(rng, amount, total, bound, skew):
    if amount == 2:
        one = jax.random.randint(rng, (), max(1, total - bound), min(bound, total - 1) + 1)
        return jnp.stack([one, total - one])
    lengths = jnp.asarray(length_profile(amount, total, bound, skew), jnp.int32)
    twos = (amount - 1) // 2
    donor, receiver = lengths[1:1 + 2 * twos:2], lengths[2:2 + 2 * twos:2]
    room = jnp.minimum(donor - 1, bound - receiver)
    passed = jax.random.randint(jax.random.fold_in(rng, 1), (twos,), 0, 1 << 20) % (room + 1)
    lengths = lengths.at[1:1 + 2 * twos:2].set(donor - passed).at[2:2 + 2 * twos:2].set(receiver + passed)
    return lengths[jax.random.permutation(jax.random.fold_in(rng, 2), amount)]


def setup_inputs(seed: int = 0, part: int = 0) -> dict:
    splits = jax.random.split(jax.random.key(seed), 10)
    part_keys = jax.random.split(jax.random.fold_in(splits[9], part), 10)
    return {
        "tiles": jnp.clip(0.00078125 * jax.random.uniform(part_keys[0], (CONS_BLOCKS, N_BLK, SLOTS_PER_BLOCK, TILE, TILE), jnp.float32) ** level_of(part_keys[0], (CONS_BLOCKS, N_BLK, SLOTS_PER_BLOCK, TILE, TILE), ((0, 4), (1, 4)), -0.2, 0.2), 0.0, 0.00078125),
        "tile_index": with_ends(jax.random.randint(part_keys[1], (CONS_BLOCKS, N_BLK, SLOTS_PER_BLOCK), 0, CBB), jax.random.fold_in(part_keys[1], 1), 0, CBB - 1).astype(jnp.int32),
        "tiles_in_use": jax.vmap(lambda own: ragged(own, N_BLK, LIVE_ROW, SLOTS_PER_BLOCK, 2))(jax.random.split(part_keys[2], CONS_BLOCKS)).reshape((CONS_BLOCKS, N_BLK)).astype(jnp.int32),
        "demand": jax.random.permutation(part_keys[3], SCEN).astype(jnp.int32),
        "profiles": draw_profiles(jax.random.fold_in(jax.random.fold_in(splits[9], part), 71), part),
        "capacity": draw_capacity(jax.random.fold_in(jax.random.fold_in(splits[9], part), 71), part),
        "start_rates": jnp.clip(1.0 * jax.random.uniform(part_keys[6], (SCEN, LINKS), jnp.float32) ** level_of(part_keys[6], (SCEN, LINKS), ((1, 4),), -0.2, 0.2), 0.0, 1.0),
        "start_duals": jnp.clip(1.0 * jax.random.uniform(part_keys[7], (SCEN, CONS), jnp.float32) ** level_of(part_keys[7], (SCEN, CONS), ((1, 4),), -0.2, 0.2), 0.0, 1.0),
        "primal_weight": jnp.clip(jnp.exp(jax.random.uniform(part_keys[8], (SCEN,), jnp.float32, math.log(0.5), math.log(2.0))), 0.5, 2.0),
    }


ETA = 0.9
EPS = 1e-06

def apply_forward_map(tiles, column_ids, live_flags, blended_rates):
    scen_count = blended_rates.shape[0]
    link_view = blended_rates.reshape(scen_count, LINK_BLOCKS, TILE)
    slot_total = N_BLK * SLOTS_PER_BLOCK

    def single_block(inputs):
        block_tiles, block_cols, block_live = inputs
        picked = link_view[:, block_cols.reshape(-1), :] * block_live.reshape(-1)[None, :, None]
        return jnp.einsum('sqj,qij->si', picked, block_tiles.reshape(slot_total, TILE, TILE), precision=lax.Precision.HIGHEST)
    block_list = lax.map(single_block, (tiles, column_ids, live_flags))
    return jnp.transpose(block_list, (1, 0, 2)).reshape(scen_count, CONS)

def apply_adjoint_map(tiles, column_ids, live_flags, dual_prices):
    scen_count = dual_prices.shape[0]
    price_reshaped = jnp.transpose(dual_prices.reshape(scen_count, CONS_BLOCKS, TILE), (1, 0, 2))
    slot_total = N_BLK * SLOTS_PER_BLOCK

    def single_block(carry, inputs):
        block_tiles, block_cols, block_live, block_prices = inputs
        contrib = jnp.einsum('si,qij->sqj', block_prices, block_tiles.reshape(slot_total, TILE, TILE), precision=lax.Precision.HIGHEST)
        contrib = contrib * block_live.reshape(-1)[None, :, None]
        return (carry.at[:, block_cols.reshape(-1), :].add(contrib), None)
    starting_point = jnp.zeros((scen_count, LINK_BLOCKS, TILE), jnp.float32)
    block_totals, discarded_value = lax.scan(single_block, starting_point, (tiles, column_ids, live_flags, price_reshaped))
    return block_totals.reshape(scen_count, LINKS)

def reference(tiles, tile_index, tiles_in_use, demand, profiles, capacity, start_rates, start_duals, primal_weight):
    column_ids = (jnp.arange(N_BLK, dtype=jnp.int32)[None, :, None] * CBB + tile_index).astype(jnp.int32)
    live_flags = (jnp.arange(SLOTS_PER_BLOCK, dtype=jnp.int32)[None, None, :] < tiles_in_use[:, :, None]).astype(jnp.float32)
    utility_weights = profiles[demand.astype(jnp.int32)]
    rates = start_rates
    duals = start_duals
    weight = primal_weight
    for iteration in range(ITERS):
        primal_step = ETA / weight
        dual_step = ETA * weight
        primal_gradient = apply_adjoint_map(tiles, column_ids, live_flags, duals) - utility_weights
        new_rates = jnp.clip(rates - primal_step[:, None] * primal_gradient, 0.0, 1.0)
        blended_rates = 2.0 * new_rates - rates
        incoming_duals = apply_forward_map(tiles, column_ids, live_flags, blended_rates)
        new_duals = jnp.maximum(0.0, duals + dual_step[:, None] * (incoming_duals - capacity))
        move_x = jnp.sqrt(lax.optimization_barrier(jnp.mean((new_rates - rates) ** 2, axis=1)) + EPS)
        move_y = jnp.sqrt(lax.optimization_barrier(jnp.mean((new_duals - duals) ** 2, axis=1)) + EPS)
        weight = jnp.sqrt(weight * move_y / move_x)
        rates = new_rates
        duals = new_duals
    return (rates, duals, weight)
```

```python
import functools

import jax
import jax.numpy as jnp
from jax import lax
from jax.experimental import pallas as pl
from jax.experimental.pallas import tpu as pltpu
from jax.sharding import PartitionSpec as P

ITERS = 3
ETA = 0.9
EPS = 1e-06
GROUPS = 2
CHUNKS = 2
Y_CHUNKS = 1
F32 = jnp.float32
BF16 = jnp.bfloat16


def split(x):
    hi = x.astype(BF16)
    return hi, (x - hi.astype(F32)).astype(BF16)


def kernel(
    rows_n, blk_n,
    tiles, tile_index, tiles_in_use, demand, profiles, capacity, start_rates, start_duals, weight_in,
    rates, duals, weight_out,
    stage, w_hi, w_lo, utility, price_split, link_split, contrib,
    z_acc, z_up, z_dn, c_send, c_recv, c_fin, y_acc, y_up, y_dn, x_move, y_move,
    load_sem, z_us, z_ur, z_ds, z_dr, y_us, y_ur, y_ds, y_dr, c_ss, c_sr, f_ss, f_sr,
    xm_ss, xm_sr, ym_ss, ym_sr,
):
    block_rows, _, slots, tile, _ = tiles.shape
    scen = profiles.shape[0]
    width = profiles.shape[1]
    dual_width = capacity.shape[1]
    blocks = width // tile
    span = scen // GROUPS
    half_rows = block_rows // 2
    total_links = width * blk_n
    total_rows = dual_width * rows_n
    z_pos = lax.axis_index("rows")
    b_pos = lax.axis_index("blk")
    y_n = blk_n // 2
    y_pos = b_pos // 2
    core = lax.rem(b_pos, 2)
    sibling = {"blk": b_pos + 1 - 2 * core}

    loads = [pltpu.make_async_copy(tiles.at[r, 0], stage.at[r], load_sem.at[r]) for r in range(block_rows)]
    for load in loads:
        load.start()

    barrier = pltpu.get_barrier_semaphore()
    for d in range(1, rows_n):
        pl.semaphore_signal(barrier, inc=1, device_id={"rows": lax.rem(z_pos + d, rows_n)}, device_id_type=pl.DeviceIdType.MESH)
    for d in range(1, blk_n):
        pl.semaphore_signal(barrier, inc=1, device_id={"blk": lax.rem(b_pos + d, blk_n)}, device_id_type=pl.DeviceIdType.MESH)

    def copy(src, dst, ss, rs, device):
        return pltpu.make_async_remote_copy(
            src_ref=src, dst_ref=dst, send_sem=ss, recv_sem=rs, device_id=device, device_id_type=pl.DeviceIdType.MESH
        )

    pending = []

    class Line:
        def __init__(self, n, pos, device, acc, up, dn, us, ur, ds, dr, chunks, count):
            self.n, self.acc, self.up, self.dn = n, acc, up, dn
            self.us, self.ur, self.ds, self.dr = us, ur, ds, dr
            self.chunks, self.size = chunks, count // chunks
            half = n // 2
            left = pos < half
            self.end = (pos == 0) | (pos == n - 1)
            self.mid = (pos == half - 1) | (pos == half)
            self.inner = device(jnp.where(left, pos + 1, pos - 1))
            self.outer = device(jnp.clip(jnp.where(left, pos - 1, pos + 1), 0, n - 1))

        def view(self, ref, b, g):
            return ref.at[b, pl.ds(g * self.size, self.size)]

        def to_mid(self, b, g):
            s = b * self.chunks + g
            return copy(self.view(self.acc, b, g), self.view(self.dn, b, g), self.us.at[s], self.dr.at[s], self.inner)

        def to_in(self, b, g):
            s = b * self.chunks + g
            return copy(self.view(self.acc, b, g), self.view(self.up, b, g), self.us.at[s], self.ur.at[s], self.inner)

        def to_out(self, b, g):
            s = b * self.chunks + g
            return copy(self.view(self.dn, b, g), self.view(self.dn, b, g), self.ds.at[s], self.dr.at[s], self.outer)

        def add(self, out, one, two, b, g):
            rows = pl.ds(g * self.size, self.size)
            out[b, rows] = one[b, rows] + two[b, rows]

        def rise(self, b, g):
            if self.n == 2:
                self.to_mid(b, g).start()
                return

            @pl.when(jnp.logical_not(self.end))
            def _():
                self.to_in(b, g).wait_recv()
                self.add(self.acc, self.acc, self.up, b, g)

            @pl.when(self.mid)
            def _():
                self.to_mid(b, g).start()

            @pl.when(jnp.logical_not(self.mid))
            def _():
                self.to_in(b, g).start()

        def fall(self, b, g):
            self.to_mid(b, g).wait_recv()
            if self.n == 2:
                self.add(self.dn, self.acc, self.dn, b, g)
                return

            @pl.when(self.mid)
            def _():
                self.add(self.dn, self.acc, self.dn, b, g)

            @pl.when(jnp.logical_not(self.end))
            def _():
                self.to_out(b, g).start()

        def drain(self, b, g):
            self.to_in(b, g).wait_send()
            if self.n > 2:

                @pl.when(jnp.logical_not(self.end))
                def _():
                    self.to_out(b, g).wait_send()

    z_line = Line(rows_n, z_pos, lambda p: {"rows": p}, z_acc, z_up, z_dn, z_us, z_ur, z_ds, z_dr, CHUNKS, blocks)
    y_line = Line(y_n, y_pos, lambda p: {"blk": 2 * p + core}, y_acc, y_up, y_dn, y_us, y_ur, y_ds, y_dr, Y_CHUNKS, half_rows)

    def scen_rows(h):
        return slice(h * span, (h + 1) * span)

    def lanes(i):
        return slice(i * tile, (i + 1) * tile)

    def lane_of(i):
        return pl.ds(pl.multiple_of(i * tile, tile), tile)

    def move_copies(buf, ss, sr, axis, pos, n, b):
        return [
            copy(buf.at[b, 0], buf.at[b, d], ss.at[b * n + d], sr.at[b * n + d], {axis: lax.rem(pos + d, n)})
            for d in range(1, n)
        ]

    def send_moves(copies):
        for c in copies:
            c.start()
            pending.append(c)

    def sum_moves(buf, copies, pos, n, b):
        for c in copies:
            c.wait_recv()
        total = None
        for j in range(n):
            part = buf[b, lax.rem(pos - j + n, n)]
            total = part if total is None else total + part
        return jnp.sum(total, axis=1, keepdims=True)

    def x_copies(b):
        return move_copies(x_move, xm_ss, xm_sr, "blk", b_pos, blk_n, b)

    def y_copies(b):
        return move_copies(y_move, ym_ss, ym_sr, "rows", z_pos, rows_n, b)

    def fold(sq):
        out = sq[:, :128]
        for i in range(1, tile // 128):
            out = out + sq[:, i * 128:(i + 1) * 128]
        return out

    weights = [weight_in[scen_rows(h), :] for h in range(GROUPS)]

    def next_weight(it, h):
        b = it * GROUPS + h
        move_x = jnp.sqrt(sum_moves(x_move, x_copies(b), b_pos, blk_n, b) / total_links + EPS)
        move_y = jnp.sqrt(sum_moves(y_move, y_copies(b), z_pos, rows_n, b) / total_rows + EPS)
        weights[h] = jnp.sqrt(weights[h] * move_y / move_x)

    def adjoint(it, h):
        b = it * GROUPS + h
        source = start_duals if it == 0 else duals
        for r in range(block_rows):
            hi, lo = split(source[scen_rows(h), lanes(r)])
            price_split[r, :span] = hi
            price_split[r, span:] = lo

        @pl.loop(0, block_rows)
        def _(r):
            lhs = price_split[r]
            for k in range(slots):
                t = r * slots + k
                main = jnp.dot(lhs, w_hi[t], preferred_element_type=F32)
                rest = jnp.dot(lhs[:span], w_lo[t], preferred_element_type=F32)
                contrib[t] = main[:span] + (main[span:] + rest)

        @pl.loop(0, blocks)
        def _(c):
            total = None
            for r in range(block_rows):
                for k in range(slots):
                    own = jnp.where(tile_index[r, 0, k] == c, 1.0, 0.0).astype(F32)
                    term = contrib[r * slots + k] * own
                    total = term if total is None else total + term
            z_acc[b, c] = total

    def rise(it, h):
        for g in range(CHUNKS):
            z_line.rise(it * GROUPS + h, g)

    def primal(it, h):
        b = it * GROUPS + h
        if it:
            next_weight(it - 1, h)
        step = ETA / weights[h]
        source = start_rates if it == 0 else rates
        moves = None
        for g in range(CHUNKS):
            z_line.fall(b, g)
            for c in range(g * z_line.size, (g + 1) * z_line.size):
                old = source[scen_rows(h), lanes(c)]
                grad = z_dn[b, c] - utility[scen_rows(h), lanes(c)]
                new = jnp.clip(old - step * grad, 0.0, 1.0)
                delta = new - old
                part = fold(delta * delta)
                moves = part if moves is None else moves + part
                rates[scen_rows(h), lanes(c)] = new
                hi, lo = split(2.0 * new - old)
                link_split[c, :span] = hi
                link_split[c, span:] = lo
        x_move[b, 0] = moves
        send_moves(x_copies(b))

    def forward_row(r):
        main = rest = None
        dims = (((1,), (1,)), ((), ()))
        for k in range(slots):
            t = r * slots + k
            lhs = link_split[tile_index[r, 0, k]]
            m = lax.dot_general(lhs, w_hi[t], dims, preferred_element_type=F32)
            e = lax.dot_general(lhs[:span], w_lo[t], dims, preferred_element_type=F32)
            main = m if main is None else main + m
            rest = e if rest is None else rest + e
        return main[:span] + (main[span:] + rest)

    def c_copy(b):
        return copy(c_send.at[b], c_recv.at[b], c_ss.at[b], c_sr.at[b], sibling)

    def f_copy(b):
        return copy(y_dn.at[b], c_fin.at[b], f_ss.at[b], f_sr.at[b], sibling)

    def forward(it, h):
        b = it * GROUPS + h

        @pl.loop(0, half_rows)
        def _(i):
            c_send[b, i] = forward_row((1 - core) * half_rows + i)

        c_copy(b).start()
        pending.append(c_copy(b))

        @pl.loop(0, half_rows)
        def _(i):
            y_acc[b, i] = forward_row(core * half_rows + i)

    def core_sum(it, h):
        b = it * GROUPS + h
        c_copy(b).wait_recv()
        y_acc[b] = y_acc[b] + c_recv[b]
        for g in range(Y_CHUNKS):
            y_line.rise(b, g)

    def y_sum(it, h):
        b = it * GROUPS + h
        for g in range(Y_CHUNKS):
            y_line.fall(b, g)
        f_copy(b).start()
        pending.append(f_copy(b))

    def dual(it, h):
        b = it * GROUPS + h
        step = ETA * weights[h]
        source = start_duals if it == 0 else duals

        def part(first, arrived):
            moves = None
            for i in range(half_rows):
                where = lane_of(first + i)
                old = source[scen_rows(h), where]
                new = jnp.maximum(0.0, old + step * (arrived[b, i] - capacity[scen_rows(h), where]))
                delta = new - old
                piece = fold(delta * delta)
                moves = piece if moves is None else moves + piece
                duals[scen_rows(h), where] = new
            return moves

        own = part(core * half_rows, y_dn)
        f_copy(b).wait_recv()
        other = part((1 - core) * half_rows, c_fin)
        y_move[b, 0] = own + other
        send_moves(y_copies(b))

    @pl.loop(0, scen)
    def _(s):
        utility[pl.ds(s, 1), :] = profiles[pl.ds(demand[s], 1), :]

    for r in range(block_rows):
        loads[r].wait()

        @pl.loop(0, slots)
        def _(k):
            live = jnp.where(k < tiles_in_use[r, 0], 1.0, 0.0).astype(F32)
            hi, lo = split(stage[r, k] * live)
            w_hi[r * slots + k] = hi
            w_lo[r * slots + k] = lo

    pl.semaphore_wait(barrier, rows_n - 1 + blk_n - 1)

    hs = range(GROUPS)
    for h in hs:
        adjoint(0, h)
        rise(0, h)
    for it in range(ITERS):
        for h in hs:
            primal(it, h)
            forward(it, h)
            if h:
                y_sum(it, h - 1)
            core_sum(it, h)
        for h in hs:
            if h == GROUPS - 1:
                y_sum(it, h)
            dual(it, h)
            if it < ITERS - 1:
                adjoint(it + 1, h)
                rise(it + 1, h)
    for h in hs:
        next_weight(ITERS - 1, h)
        weight_out[scen_rows(h), :] = weights[h]

    for c in pending:
        c.wait_send()
    for b in range(ITERS * GROUPS):
        for g in range(CHUNKS):
            z_line.drain(b, g)
        for g in range(Y_CHUNKS):
            y_line.drain(b, g)


def body(tiles, tile_index, tiles_in_use, demand, profiles, capacity, start_rates, start_duals, primal_weight):
    rows_n = lax.axis_size("rows")
    blk_n = lax.axis_size("blk")
    block_rows, _, slots, tile, _ = tiles.shape
    scen, width = profiles.shape
    dual_width = capacity.shape[1]
    blocks = width // tile
    span = scen // GROUPS
    nb = ITERS * GROUPS
    half = block_rows // 2
    vmem = pl.BlockSpec(memory_space=pltpu.VMEM)
    smem = pl.BlockSpec(memory_space=pltpu.SMEM)
    dma = pltpu.SemaphoreType.DMA
    z_buf = pltpu.VMEM((nb, blocks, span, tile), F32)
    y_buf = pltpu.VMEM((nb, half, span, tile), F32)
    rates, duals, weight = pl.pallas_call(
        functools.partial(kernel, rows_n, blk_n),
        out_shape=(
            jax.ShapeDtypeStruct((scen, width), F32),
            jax.ShapeDtypeStruct((scen, dual_width), F32),
            jax.ShapeDtypeStruct((scen, 1), F32),
        ),
        in_specs=[pl.BlockSpec(memory_space=pl.ANY), smem, smem, smem, vmem, vmem, vmem, vmem, vmem],
        out_specs=(vmem, vmem, vmem),
        scratch_shapes=[
            pltpu.VMEM((block_rows, slots, tile, tile), F32),
            pltpu.VMEM((block_rows * slots, tile, tile), BF16),
            pltpu.VMEM((block_rows * slots, tile, tile), BF16),
            pltpu.VMEM((scen, width), F32),
            pltpu.VMEM((block_rows, 2 * span, tile), BF16),
            pltpu.VMEM((blocks, 2 * span, tile), BF16),
            pltpu.VMEM((block_rows * slots, span, tile), F32),
            z_buf, z_buf, z_buf,
            y_buf, y_buf, y_buf, y_buf, y_buf, y_buf,
            pltpu.VMEM((nb, blk_n, span, 128), F32),
            pltpu.VMEM((nb, rows_n, span, 128), F32),
            dma((block_rows,)),
            dma((nb * CHUNKS,)), dma((nb * CHUNKS,)), dma((nb * CHUNKS,)), dma((nb * CHUNKS,)),
            dma((nb * Y_CHUNKS,)), dma((nb * Y_CHUNKS,)), dma((nb * Y_CHUNKS,)), dma((nb * Y_CHUNKS,)),
            dma((nb,)), dma((nb,)), dma((nb,)), dma((nb,)),
            dma((nb * blk_n,)), dma((nb * blk_n,)), dma((nb * rows_n,)), dma((nb * rows_n,)),
        ],
        compiler_params=pltpu.CompilerParams(
            collective_id=0, has_side_effects=True, vmem_limit_bytes=60 * 1024 * 1024
        ),
    )(
        tiles, tile_index, tiles_in_use, demand, profiles, capacity, start_rates, start_duals,
        primal_weight[:, None],
    )
    return rates, duals, weight[:, 0]


def solution(mesh):
    placed = (
        P(("groups", "rows"), "blk", None, None, None),
        P(("groups", "rows"), "blk", None),
        P(("groups", "rows"), "blk"),
        P("groups"),
        P("groups", "blk"),
        P("groups", "rows"),
        P("groups", "blk"),
        P("groups", "rows"),
        P("groups"),
    )
    return jax.shard_map(
        body,
        mesh=mesh,
        in_specs=placed,
        out_specs=(P("groups", "blk"), P("groups", "rows"), P("groups")),
        check_vma=False,
    )
```

```python
import functools

import jax
import jax.numpy as jnp
from jax import lax
from jax.experimental import pallas as pl
from jax.experimental.pallas import tpu as pltpu
from jax.sharding import PartitionSpec as P

ITERS = 3
ETA = 0.9
EPS = 1e-06
GROUPS = 2
CHUNKS = 4
Y_CHUNKS = 1
F32 = jnp.float32
BF16 = jnp.bfloat16


def split(x):
    hi = x.astype(BF16)
    return hi, (x - hi.astype(F32)).astype(BF16)


def kernel(
    rows_n, blk_n,
    tiles, tile_index_in, tiles_in_use_in, demand, profiles, capacity, start_rates, start_duals, weight_in,
    rates, duals, weight_out,
    stage, w_hi, w_lo, t_hi, t_lo, utility, weight_col, tile_index, tiles_in_use, link_split, contrib,
    z_acc, z_up, z_dn, c_send, c_recv, c_fin, y_acc, y_up, y_dn, x_move, y_move,
    load_sem, table_sem, z_us, z_ur, z_ds, z_dr, y_us, y_ur, y_ds, y_dr, c_ss, c_sr, f_ss, f_sr,
    xm_ss, xm_sr, ym_ss, ym_sr,
):
    block_rows, _, slots, tile, _ = tiles.shape
    scen = profiles.shape[0]
    width = profiles.shape[1]
    dual_width = capacity.shape[1]
    blocks = width // tile
    span = scen // GROUPS
    half_rows = block_rows // 2
    total_links = width * blk_n
    total_rows = dual_width * rows_n
    z_pos = lax.axis_index("rows")
    b_pos = lax.axis_index("blk")
    y_n = blk_n // 2
    y_pos = b_pos // 2
    core = lax.rem(b_pos, 2)
    sibling = {"blk": b_pos + 1 - 2 * core}

    loads = [pltpu.make_async_copy(tiles.at[r, 0], stage.at[r], load_sem.at[r]) for r in range(block_rows)]
    tables = [
        pltpu.make_async_copy(tile_index_in, tile_index, table_sem.at[0]),
        pltpu.make_async_copy(tiles_in_use_in, tiles_in_use, table_sem.at[1]),
    ]
    for load in tables + loads:
        load.start()

    barrier = pltpu.get_barrier_semaphore()
    for d in range(1, rows_n):
        pl.semaphore_signal(barrier, inc=1, device_id={"rows": lax.rem(z_pos + d, rows_n)}, device_id_type=pl.DeviceIdType.MESH)
    for d in range(1, blk_n):
        pl.semaphore_signal(barrier, inc=1, device_id={"blk": lax.rem(b_pos + d, blk_n)}, device_id_type=pl.DeviceIdType.MESH)

    def copy(src, dst, ss, rs, device):
        return pltpu.make_async_remote_copy(
            src_ref=src, dst_ref=dst, send_sem=ss, recv_sem=rs, device_id=device, device_id_type=pl.DeviceIdType.MESH
        )

    pending = []

    class Line:
        def __init__(self, n, pos, device, acc, up, dn, us, ur, ds, dr, chunks, count):
            self.n, self.acc, self.up, self.dn = n, acc, up, dn
            self.us, self.ur, self.ds, self.dr = us, ur, ds, dr
            self.chunks, self.size = chunks, count // chunks
            half = n // 2
            left = pos < half
            self.end = (pos == 0) | (pos == n - 1)
            self.mid = (pos == half - 1) | (pos == half)
            self.inner = device(jnp.where(left, pos + 1, pos - 1))
            self.outer = device(jnp.clip(jnp.where(left, pos - 1, pos + 1), 0, n - 1))

        def view(self, ref, b, g):
            return ref.at[b, pl.ds(g * self.size, self.size)]

        def to_mid(self, b, g):
            s = b * self.chunks + g
            return copy(self.view(self.acc, b, g), self.view(self.dn, b, g), self.us.at[s], self.dr.at[s], self.inner)

        def to_in(self, b, g):
            s = b * self.chunks + g
            return copy(self.view(self.acc, b, g), self.view(self.up, b, g), self.us.at[s], self.ur.at[s], self.inner)

        def to_out(self, b, g):
            s = b * self.chunks + g
            return copy(self.view(self.dn, b, g), self.view(self.dn, b, g), self.ds.at[s], self.dr.at[s], self.outer)

        def add(self, out, one, two, b, g):
            rows = pl.ds(g * self.size, self.size)
            out[b, rows] = one[b, rows] + two[b, rows]

        def launch(self, b, g):
            if self.n == 2:
                self.to_mid(b, g).start()
                return

            @pl.when(self.end)
            def _():
                self.to_in(b, g).start()

        def rise(self, b, g):
            if self.n == 2:
                return

            @pl.when(jnp.logical_not(self.end))
            def _():
                self.to_in(b, g).wait_recv()
                self.add(self.acc, self.acc, self.up, b, g)

            @pl.when(self.mid)
            def _():
                self.to_mid(b, g).start()

            if self.n > 4:

                @pl.when(jnp.logical_not(self.mid | self.end))
                def _():
                    self.to_in(b, g).start()

        def fall(self, b, g):
            self.to_mid(b, g).wait_recv()
            if self.n == 2:
                self.add(self.dn, self.acc, self.dn, b, g)
                return

            @pl.when(self.mid)
            def _():
                self.add(self.dn, self.acc, self.dn, b, g)

            @pl.when(jnp.logical_not(self.end))
            def _():
                self.to_out(b, g).start()

        def drain(self, b, g):
            self.to_in(b, g).wait_send()
            if self.n > 2:

                @pl.when(jnp.logical_not(self.end))
                def _():
                    self.to_out(b, g).wait_send()

    z_line = Line(rows_n, z_pos, lambda p: {"rows": p}, z_acc, z_up, z_dn, z_us, z_ur, z_ds, z_dr, CHUNKS, blocks)
    y_line = Line(y_n, y_pos, lambda p: {"blk": 2 * p + core}, y_acc, y_up, y_dn, y_us, y_ur, y_ds, y_dr, Y_CHUNKS, half_rows)

    def scen_rows(h):
        return slice(h * span, (h + 1) * span)

    def lanes(i):
        return slice(i * tile, (i + 1) * tile)

    def lane_of(i):
        return pl.ds(pl.multiple_of(i * tile, tile), tile)

    def move_copies(buf, ss, sr, axis, pos, n, b):
        return [
            copy(buf.at[b, 0], buf.at[b, d], ss.at[b * n + d], sr.at[b * n + d], {axis: lax.rem(pos + d, n)})
            for d in range(1, n)
        ]

    def send_moves(copies):
        for c in copies:
            c.start()
            pending.append(c)

    def sum_moves(buf, copies, pos, n, b):
        for c in copies:
            c.wait_recv()
        total = None
        for j in range(n):
            part = buf[b, lax.rem(pos - j + n, n)]
            total = part if total is None else total + part
        return jnp.sum(total, axis=1, keepdims=True)

    def x_copies(b):
        return move_copies(x_move, xm_ss, xm_sr, "blk", b_pos, blk_n, b)

    def y_copies(b):
        return move_copies(y_move, ym_ss, ym_sr, "rows", z_pos, rows_n, b)

    def fold(sq):
        out = sq[:, :128]
        for i in range(1, tile // 128):
            out = out + sq[:, i * 128:(i + 1) * 128]
        return out

    weights = []

    def next_weight(it, h):
        b = it * GROUPS + h
        move_x = jnp.sqrt(sum_moves(x_move, x_copies(b), b_pos, blk_n, b) / total_links + EPS)
        move_y = jnp.sqrt(sum_moves(y_move, y_copies(b), z_pos, rows_n, b) / total_rows + EPS)
        weights[h] = jnp.sqrt(weights[h] * move_y / move_x)

    def price_rows(it, h, first, count):
        source = start_duals if it == 0 else duals

        @pl.loop(first, first + count)
        def _(r):
            hi, lo = split(source[scen_rows(h), lane_of(r)])
            lhs = jnp.concatenate([hi, lo], axis=0)
            for k in range(slots):
                t = r * slots + k
                main = jnp.dot(lhs, w_hi[t], preferred_element_type=F32)
                rest = jnp.dot(hi, w_lo[t], preferred_element_type=F32)
                contrib[t] = main[:span] + (main[span:] + rest)

    def scatter(it, h):
        b = it * GROUPS + h
        for g in range(CHUNKS):

            @pl.loop(g * z_line.size, (g + 1) * z_line.size)
            def _(c):
                total = None
                for r in range(block_rows):
                    for k in range(slots):
                        own = jnp.where(tile_index[k, r] == c, 1.0, 0.0).astype(F32)
                        term = contrib[r * slots + k] * own
                        total = term if total is None else total + term
                z_acc[b, c] = total

            z_line.launch(b, g)

    def rise(it, h, g):
        z_line.rise(it * GROUPS + h, g)

    moves_of = {}

    def primal(it, h, g):
        b = it * GROUPS + h
        if it and g == 0:
            next_weight(it - 1, h)
        step = ETA / weights[h]
        source = start_rates if it == 0 else rates
        z_line.fall(b, g)
        moves = moves_of.get(b)
        for c in range(g * z_line.size, (g + 1) * z_line.size):
            old = source[scen_rows(h), lanes(c)]
            grad = z_dn[b, c] - utility[scen_rows(h), lanes(c)]
            new = jnp.clip(old - step * grad, 0.0, 1.0)
            delta = new - old
            part = fold(delta * delta)
            moves = part if moves is None else moves + part
            rates[scen_rows(h), lanes(c)] = new
            hi, lo = split(2.0 * new - old)
            link_split[h, c, :span] = hi
            link_split[h, c, span:] = lo
        moves_of[b] = moves
        if g == CHUNKS - 1:
            x_move[b, 0] = moves
            send_moves(x_copies(b))

    def transpose_rows(first, count):
        @pl.loop(first * slots, (first + count) * slots)
        def _(t):
            t_hi[t] = w_hi[t].T
            t_lo[t] = w_lo[t].T

    def forward_row(h, r):
        main = rest = None
        for k in range(slots):
            t = r * slots + k
            lhs = link_split[h, tile_index[k, r]]
            m = jnp.dot(lhs, t_hi[t], preferred_element_type=F32)
            e = jnp.dot(lhs[:span], t_lo[t], preferred_element_type=F32)
            main = m if main is None else main + m
            rest = e if rest is None else rest + e
        return main[:span] + (main[span:] + rest)

    def c_copy(b):
        return copy(c_send.at[b], c_recv.at[b], c_ss.at[b], c_sr.at[b], sibling)

    def f_copy(b):
        return copy(y_dn.at[b], c_fin.at[b], f_ss.at[b], f_sr.at[b], sibling)

    def forward_far(it, h, first, count):
        b = it * GROUPS + h

        @pl.loop(first, first + count)
        def _(i):
            c_send[b, i] = forward_row(h, (1 - core) * half_rows + i)

        if first + count == half_rows:
            c_copy(b).start()
            pending.append(c_copy(b))

    def forward_near(it, h, first, count):
        b = it * GROUPS + h

        @pl.loop(first, first + count)
        def _(i):
            y_acc[b, i] = forward_row(h, core * half_rows + i)

    def core_sum(it, h):
        b = it * GROUPS + h
        c_copy(b).wait_recv()
        y_acc[b] = y_acc[b] + c_recv[b]
        for g in range(Y_CHUNKS):
            y_line.launch(b, g)
        for g in range(Y_CHUNKS):
            y_line.rise(b, g)

    def y_sum(it, h):
        b = it * GROUPS + h
        for g in range(Y_CHUNKS):
            y_line.fall(b, g)
        f_copy(b).start()
        pending.append(f_copy(b))

    def dual(it, h):
        b = it * GROUPS + h
        step = ETA * weights[h]
        source = start_duals if it == 0 else duals

        def part(first, arrived):
            moves = None
            for i in range(half_rows):
                where = lane_of(first + i)
                old = source[scen_rows(h), where]
                new = jnp.maximum(0.0, old + step * (arrived[b, i] - capacity[scen_rows(h), where]))
                delta = new - old
                piece = fold(delta * delta)
                moves = piece if moves is None else moves + piece
                duals[scen_rows(h), where] = new
            return moves

        own = part(core * half_rows, y_dn)
        f_copy(b).wait_recv()
        other = part((1 - core) * half_rows, c_fin)
        y_move[b, 0] = own + other
        send_moves(y_copies(b))

    @pl.loop(0, scen)
    def _(s):
        utility[pl.ds(s, 1), :] = profiles[pl.ds(demand[s], 1), :]
        weight_col[pl.ds(s, 1), :] = jnp.full((1, 128), weight_in[s], F32)

    for h in range(GROUPS):
        weights.append(weight_col[scen_rows(h), :1])
    for table in tables:
        table.wait()

    for r in range(block_rows):
        loads[r].wait()

        @pl.loop(0, slots)
        def _(k):
            live = jnp.where(k < tiles_in_use[0, r], 1.0, 0.0).astype(F32)
            hi, lo = split(stage[r, k] * live)
            w_hi[r * slots + k] = hi
            w_lo[r * slots + k] = lo

    pl.semaphore_wait(barrier, rows_n - 1 + blk_n - 1)

    quarter = block_rows // 4
    eighth = half_rows // 2
    price_rows(0, 0, 0, block_rows)
    scatter(0, 0)
    price_rows(0, 1, 0, block_rows)
    for it in range(ITERS):
        rise(it, 0, 0)
        scatter(it, 1)

        def fill(i):
            if it == 0:
                transpose_rows(i * quarter, quarter)

        fill(0)
        rise(it, 0, 1)
        fill(1)
        rise(it, 0, 2)
        primal(it, 0, 0)
        fill(2)
        rise(it, 0, 3)
        primal(it, 0, 1)
        fill(3)
        rise(it, 1, 0)
        primal(it, 0, 2)
        primal(it, 0, 3)
        forward_far(it, 0, 0, eighth)
        rise(it, 1, 1)
        forward_far(it, 0, eighth, eighth)
        rise(it, 1, 2)
        primal(it, 1, 0)
        forward_near(it, 0, 0, eighth)
        rise(it, 1, 3)
        primal(it, 1, 1)
        forward_near(it, 0, eighth, eighth)
        core_sum(it, 0)
        primal(it, 1, 2)
        primal(it, 1, 3)
        forward_far(it, 1, 0, half_rows)
        forward_near(it, 1, 0, eighth)
        y_sum(it, 0)
        forward_near(it, 1, eighth, eighth)
        core_sum(it, 1)
        dual(it, 0)
        last = it == ITERS - 1
        if not last:
            price_rows(it + 1, 0, 0, block_rows)
        y_sum(it, 1)
        if not last:
            scatter(it + 1, 0)
        dual(it, 1)
        if not last:
            price_rows(it + 1, 1, 0, block_rows)
    for h in range(GROUPS):
        next_weight(ITERS - 1, h)
        weight_out[scen_rows(h), :] = jnp.broadcast_to(weights[h], (span, 128))

    for c in pending:
        c.wait_send()
    for b in range(ITERS * GROUPS):
        for g in range(CHUNKS):
            z_line.drain(b, g)
        for g in range(Y_CHUNKS):
            y_line.drain(b, g)


def finish(rates, duals, weight, rates_out, duals_out, weight_out):
    rates_out[...] = rates[...]
    duals_out[...] = duals[...]
    scen = weight_out.shape[0]
    shape = weight.shape
    here = lax.broadcasted_iota(jnp.int32, shape, 0) == lax.broadcasted_iota(jnp.int32, shape, 1)
    weight_out[...] = jnp.sum(jnp.where(here, weight[...], 0.0), axis=0)[:scen]


def body(tiles, tile_index, tiles_in_use, demand, profiles, capacity, start_rates, start_duals, primal_weight):
    rows_n = lax.axis_size("rows")
    blk_n = lax.axis_size("blk")
    block_rows, _, slots, tile, _ = tiles.shape
    scen, width = profiles.shape
    dual_width = capacity.shape[1]
    blocks = width // tile
    span = scen // GROUPS
    nb = ITERS * GROUPS
    half = block_rows // 2
    vmem = pl.BlockSpec(memory_space=pltpu.VMEM)
    smem = pl.BlockSpec(memory_space=pltpu.SMEM)
    hbm = pl.BlockSpec(memory_space=pl.ANY)
    dma = pltpu.SemaphoreType.DMA
    w_buf = pltpu.VMEM((block_rows * slots, tile, tile), BF16)
    z_buf = pltpu.VMEM((nb, blocks, span, tile), F32)
    y_buf = pltpu.VMEM((nb, half, span, tile), F32)
    rates, duals, weight = pl.pallas_call(
        functools.partial(kernel, rows_n, blk_n),
        out_shape=(
            jax.ShapeDtypeStruct((scen, width), F32),
            jax.ShapeDtypeStruct((scen, dual_width), F32),
            jax.ShapeDtypeStruct((scen, 128), F32),
        ),
        in_specs=[hbm, hbm, hbm, smem, vmem, vmem, vmem, vmem, smem],
        out_specs=(vmem, vmem, vmem),
        scratch_shapes=[
            pltpu.VMEM((block_rows, slots, tile, tile), F32),
            w_buf, w_buf, w_buf, w_buf,
            pltpu.VMEM((scen, width), F32),
            pltpu.VMEM((scen, 128), F32),
            pltpu.SMEM((slots, block_rows), jnp.int32),
            pltpu.SMEM((1, block_rows), jnp.int32),
            pltpu.VMEM((GROUPS, blocks, 2 * span, tile), BF16),
            pltpu.VMEM((block_rows * slots, span, tile), F32),
            z_buf, z_buf, z_buf,
            y_buf, y_buf, y_buf, y_buf, y_buf, y_buf,
            pltpu.VMEM((nb, blk_n, span, 128), F32),
            pltpu.VMEM((nb, rows_n, span, 128), F32),
            dma((block_rows,)), dma((2,)),
            dma((nb * CHUNKS,)), dma((nb * CHUNKS,)), dma((nb * CHUNKS,)), dma((nb * CHUNKS,)),
            dma((nb * Y_CHUNKS,)), dma((nb * Y_CHUNKS,)), dma((nb * Y_CHUNKS,)), dma((nb * Y_CHUNKS,)),
            dma((nb,)), dma((nb,)), dma((nb,)), dma((nb,)),
            dma((nb * blk_n,)), dma((nb * blk_n,)), dma((nb * rows_n,)), dma((nb * rows_n,)),
        ],
        compiler_params=pltpu.CompilerParams(
            collective_id=0, has_side_effects=True, vmem_limit_bytes=60 * 1024 * 1024
        ),
    )(
        tiles, tile_index[:, 0].T, tiles_in_use.T, demand, profiles, capacity, start_rates, start_duals,
        primal_weight,
    )
    return pl.pallas_call(
        finish,
        out_shape=(
            jax.ShapeDtypeStruct(rates.shape, F32),
            jax.ShapeDtypeStruct(duals.shape, F32),
            jax.ShapeDtypeStruct((scen,), F32),
        ),
        in_specs=[vmem, vmem, vmem],
        out_specs=(vmem, vmem, vmem),
    )(rates, duals, weight)


def solution(mesh):
    placed = (
        P(("groups", "rows"), "blk", None, None, None),
        P(("groups", "rows"), "blk", None),
        P(("groups", "rows"), "blk"),
        P("groups"),
        P("groups", "blk"),
        P("groups", "rows"),
        P("groups", "blk"),
        P("groups", "rows"),
        P("groups"),
    )
    return jax.shard_map(
        body,
        mesh=mesh,
        in_specs=placed,
        out_specs=(P("groups", "blk"), P("groups", "rows"), P("groups")),
        check_vma=False,
    )
```

```python
import functools

import jax
import jax.numpy as jnp
from jax import lax
from jax.experimental import pallas as pl
from jax.experimental.pallas import tpu as pltpu
from jax.sharding import PartitionSpec as P

ITERS = 3
ETA = 0.9
EPS = 1e-06
GROUPS = 2
CHUNKS = 4
Y_CHUNKS = 2
F32 = jnp.float32
BF16 = jnp.bfloat16


def split(x):
    hi = x.astype(BF16)
    return hi, (x - hi.astype(F32)).astype(BF16)


def kernel(
    rows_n, blk_n,
    tiles, tile_index_in, tiles_in_use_in, demand, profiles, capacity, start_rates, start_duals, weight_in,
    rates, duals, weight_out,
    stage, w_hi, w_lo, t_hi, t_lo, utility, weight_col, tile_index, tiles_in_use, link_split, contrib,
    z_acc, z_up, z_dn, c_send, c_recv, c_fin, y_acc, y_up, y_dn, x_move, y_move,
    load_sem, table_sem, z_us, z_ur, z_ds, z_dr, y_us, y_ur, y_ds, y_dr, c_ss, c_sr, f_ss, f_sr,
    xm_ss, xm_sr, ym_ss, ym_sr,
):
    block_rows, _, slots, tile, _ = tiles.shape
    scen = profiles.shape[0]
    width = profiles.shape[1]
    dual_width = capacity.shape[1]
    blocks = width // tile
    span = scen // GROUPS
    half_rows = block_rows // 2
    total_links = width * blk_n
    total_rows = dual_width * rows_n
    z_pos = lax.axis_index("rows")
    b_pos = lax.axis_index("blk")
    y_n = blk_n // 2
    y_pos = b_pos // 2
    core = lax.rem(b_pos, 2)
    sibling = {"blk": b_pos + 1 - 2 * core}

    loads = [pltpu.make_async_copy(tiles.at[r, 0], stage.at[r], load_sem.at[r]) for r in range(block_rows)]
    tables = [
        pltpu.make_async_copy(tile_index_in, tile_index, table_sem.at[0]),
        pltpu.make_async_copy(tiles_in_use_in, tiles_in_use, table_sem.at[1]),
    ]
    for load in tables + loads:
        load.start()

    barrier = pltpu.get_barrier_semaphore()
    for d in range(1, rows_n):
        pl.semaphore_signal(barrier, inc=1, device_id={"rows": lax.rem(z_pos + d, rows_n)}, device_id_type=pl.DeviceIdType.MESH)
    for d in range(1, blk_n):
        pl.semaphore_signal(barrier, inc=1, device_id={"blk": lax.rem(b_pos + d, blk_n)}, device_id_type=pl.DeviceIdType.MESH)

    def copy(src, dst, ss, rs, device):
        return pltpu.make_async_remote_copy(
            src_ref=src, dst_ref=dst, send_sem=ss, recv_sem=rs, device_id=device, device_id_type=pl.DeviceIdType.MESH
        )

    pending = []

    class Line:
        def __init__(self, n, pos, device, acc, up, dn, us, ur, ds, dr, chunks, count):
            self.n, self.acc, self.up, self.dn = n, acc, up, dn
            self.us, self.ur, self.ds, self.dr = us, ur, ds, dr
            self.chunks, self.size = chunks, count // chunks
            half = n // 2
            left = pos < half
            self.end = (pos == 0) | (pos == n - 1)
            self.mid = (pos == half - 1) | (pos == half)
            self.inner = device(jnp.where(left, pos + 1, pos - 1))
            self.outer = device(jnp.clip(jnp.where(left, pos - 1, pos + 1), 0, n - 1))

        def view(self, ref, b, g):
            return ref.at[b, pl.ds(g * self.size, self.size)]

        def to_mid(self, b, g):
            s = b * self.chunks + g
            return copy(self.view(self.acc, b, g), self.view(self.dn, b, g), self.us.at[s], self.dr.at[s], self.inner)

        def to_in(self, b, g):
            s = b * self.chunks + g
            return copy(self.view(self.acc, b, g), self.view(self.up, b, g), self.us.at[s], self.ur.at[s], self.inner)

        def to_out(self, b, g):
            s = b * self.chunks + g
            return copy(self.view(self.dn, b, g), self.view(self.dn, b, g), self.ds.at[s], self.dr.at[s], self.outer)

        def add(self, out, one, two, b, g):
            rows = pl.ds(g * self.size, self.size)
            out[b, rows] = one[b, rows] + two[b, rows]

        def launch(self, b, g):
            if self.n == 2:
                self.to_mid(b, g).start()
                return

            @pl.when(self.end)
            def _():
                self.to_in(b, g).start()

        def rise(self, b, g):
            if self.n == 2:
                return

            @pl.when(jnp.logical_not(self.end))
            def _():
                self.to_in(b, g).wait_recv()
                self.add(self.acc, self.acc, self.up, b, g)

            @pl.when(self.mid)
            def _():
                self.to_mid(b, g).start()

            if self.n > 4:

                @pl.when(jnp.logical_not(self.mid | self.end))
                def _():
                    self.to_in(b, g).start()

        def fall(self, b, g):
            self.to_mid(b, g).wait_recv()
            if self.n == 2:
                self.add(self.dn, self.acc, self.dn, b, g)
                return

            @pl.when(self.mid)
            def _():
                self.add(self.dn, self.acc, self.dn, b, g)

            @pl.when(jnp.logical_not(self.end))
            def _():
                self.to_out(b, g).start()

        def drain(self, b, g):
            self.to_in(b, g).wait_send()
            if self.n > 2:

                @pl.when(jnp.logical_not(self.end))
                def _():
                    self.to_out(b, g).wait_send()

    z_line = Line(rows_n, z_pos, lambda p: {"rows": p}, z_acc, z_up, z_dn, z_us, z_ur, z_ds, z_dr, CHUNKS, blocks)
    y_line = Line(y_n, y_pos, lambda p: {"blk": 2 * p + core}, y_acc, y_up, y_dn, y_us, y_ur, y_ds, y_dr, Y_CHUNKS, half_rows)

    def scen_rows(h):
        return slice(h * span, (h + 1) * span)

    def lanes(i):
        return slice(i * tile, (i + 1) * tile)

    def lane_of(i):
        return pl.ds(pl.multiple_of(i * tile, tile), tile)

    def move_copies(buf, ss, sr, axis, pos, n, b):
        return [
            copy(buf.at[b, 0], buf.at[b, d], ss.at[b * n + d], sr.at[b * n + d], {axis: lax.rem(pos + d, n)})
            for d in range(1, n)
        ]

    def send_moves(copies):
        for c in copies:
            c.start()
            pending.append(c)

    def sum_moves(buf, copies, pos, n, b):
        for c in copies:
            c.wait_recv()
        total = None
        for j in range(n):
            part = buf[b, lax.rem(pos - j + n, n)]
            total = part if total is None else total + part
        return jnp.sum(total, axis=1, keepdims=True)

    def x_copies(b):
        return move_copies(x_move, xm_ss, xm_sr, "blk", b_pos, blk_n, b)

    def y_copies(b):
        return move_copies(y_move, ym_ss, ym_sr, "rows", z_pos, rows_n, b)

    def fold(sq):
        out = sq[:, :128]
        for i in range(1, tile // 128):
            out = out + sq[:, i * 128:(i + 1) * 128]
        return out

    weights = []

    def next_weight(it, h):
        b = it * GROUPS + h
        move_x = jnp.sqrt(sum_moves(x_move, x_copies(b), b_pos, blk_n, b) / total_links + EPS)
        move_y = jnp.sqrt(sum_moves(y_move, y_copies(b), z_pos, rows_n, b) / total_rows + EPS)
        weights[h] = jnp.sqrt(weights[h] * move_y / move_x)

    def price_rows(it, h, first, count):
        source = start_duals if it == 0 else duals

        @pl.loop(first, first + count)
        def _(r):
            hi, lo = split(source[scen_rows(h), lane_of(r)])
            lhs = jnp.concatenate([hi, lo], axis=0)
            for k in range(slots):
                t = r * slots + k
                main = jnp.dot(lhs, w_hi[t], preferred_element_type=F32)
                rest = jnp.dot(hi, w_lo[t], preferred_element_type=F32)
                contrib[t] = main[:span] + (main[span:] + rest)

    def scatter(it, h):
        b = it * GROUPS + h
        for g in range(CHUNKS):

            @pl.loop(g * z_line.size, (g + 1) * z_line.size)
            def _(c):
                total = None
                for r in range(block_rows):
                    for k in range(slots):
                        own = jnp.where(tile_index[k, r] == c, 1.0, 0.0).astype(F32)
                        term = contrib[r * slots + k] * own
                        total = term if total is None else total + term
                z_acc[b, c] = total

            z_line.launch(b, g)

    def rise(it, h, g):
        z_line.rise(it * GROUPS + h, g)

    moves_of = {}

    def primal(it, h, g):
        b = it * GROUPS + h
        if it and g == 0:
            next_weight(it - 1, h)
        step = ETA / weights[h]
        source = start_rates if it == 0 else rates
        z_line.fall(b, g)
        moves = moves_of.get(b)
        for c in range(g * z_line.size, (g + 1) * z_line.size):
            old = source[scen_rows(h), lanes(c)]
            grad = z_dn[b, c] - utility[scen_rows(h), lanes(c)]
            new = jnp.clip(old - step * grad, 0.0, 1.0)
            delta = new - old
            part = fold(delta * delta)
            moves = part if moves is None else moves + part
            rates[scen_rows(h), lanes(c)] = new
            hi, lo = split(2.0 * new - old)
            link_split[h, c, :span] = hi
            link_split[h, c, span:] = lo
        moves_of[b] = moves
        if g == CHUNKS - 1:
            x_move[b, 0] = moves
            send_moves(x_copies(b))

    def transpose_rows(first, count):
        @pl.loop(first * slots, (first + count) * slots)
        def _(t):
            t_hi[t] = w_hi[t].T
            t_lo[t] = w_lo[t].T

    def forward_row(h, r):
        main = rest = None
        for k in range(slots):
            t = r * slots + k
            lhs = link_split[h, tile_index[k, r]]
            m = jnp.dot(lhs, t_hi[t], preferred_element_type=F32)
            e = jnp.dot(lhs[:span], t_lo[t], preferred_element_type=F32)
            main = m if main is None else main + m
            rest = e if rest is None else rest + e
        return main[:span] + (main[span:] + rest)

    y_size = half_rows // Y_CHUNKS

    def c_copy(b, g):
        rows, s = pl.ds(g * y_size, y_size), b * Y_CHUNKS + g
        return copy(c_send.at[b, rows], c_recv.at[b, rows], c_ss.at[s], c_sr.at[s], sibling)

    def f_copy(b, g):
        rows, s = pl.ds(g * y_size, y_size), b * Y_CHUNKS + g
        return copy(y_dn.at[b, rows], c_fin.at[b, rows], f_ss.at[s], f_sr.at[s], sibling)

    def forward_far(it, h, g):
        b = it * GROUPS + h

        @pl.loop(g * y_size, (g + 1) * y_size)
        def _(i):
            c_send[b, i] = forward_row(h, (1 - core) * half_rows + i)

        c_copy(b, g).start()
        pending.append(c_copy(b, g))

    def forward_near(it, h, g):
        b = it * GROUPS + h

        @pl.loop(g * y_size, (g + 1) * y_size)
        def _(i):
            y_acc[b, i] = forward_row(h, core * half_rows + i)

        c_copy(b, g).wait_recv()
        y_line.add(y_acc, y_acc, c_recv, b, g)
        y_line.launch(b, g)
        y_line.rise(b, g)

    def y_sum(it, h, g):
        b = it * GROUPS + h
        y_line.fall(b, g)
        f_copy(b, g).start()
        pending.append(f_copy(b, g))

    def dual(it, h):
        b = it * GROUPS + h
        step = ETA * weights[h]
        source = start_duals if it == 0 else duals

        def part(first, arrived):
            moves = None
            for i in range(half_rows):
                where = lane_of(first + i)
                old = source[scen_rows(h), where]
                new = jnp.maximum(0.0, old + step * (arrived[b, i] - capacity[scen_rows(h), where]))
                delta = new - old
                piece = fold(delta * delta)
                moves = piece if moves is None else moves + piece
                duals[scen_rows(h), where] = new
            return moves

        own = part(core * half_rows, y_dn)
        for g in range(Y_CHUNKS):
            f_copy(b, g).wait_recv()
        other = part((1 - core) * half_rows, c_fin)
        y_move[b, 0] = own + other
        send_moves(y_copies(b))

    @pl.loop(0, scen)
    def _(s):
        utility[pl.ds(s, 1), :] = profiles[pl.ds(demand[s], 1), :]
        weight_col[pl.ds(s, 1), :] = jnp.full((1, 128), weight_in[s], F32)

    for h in range(GROUPS):
        weights.append(weight_col[scen_rows(h), :1])
    for table in tables:
        table.wait()

    for r in range(block_rows):
        loads[r].wait()

        @pl.loop(0, slots)
        def _(k):
            live = jnp.where(k < tiles_in_use[0, r], 1.0, 0.0).astype(F32)
            hi, lo = split(stage[r, k] * live)
            w_hi[r * slots + k] = hi
            w_lo[r * slots + k] = lo

    pl.semaphore_wait(barrier, rows_n - 1 + blk_n - 1)

    quarter = block_rows // 4
    price_rows(0, 0, 0, block_rows)
    scatter(0, 0)
    price_rows(0, 1, 0, block_rows)
    for it in range(ITERS):
        rise(it, 0, 0)
        scatter(it, 1)

        def fill(i):
            if it == 0:
                transpose_rows(i * quarter, quarter)

        fill(0)
        rise(it, 0, 1)
        fill(1)
        rise(it, 0, 2)
        primal(it, 0, 0)
        fill(2)
        rise(it, 0, 3)
        primal(it, 0, 1)
        fill(3)
        rise(it, 1, 0)
        primal(it, 0, 2)
        primal(it, 0, 3)
        forward_far(it, 0, 0)
        rise(it, 1, 1)
        forward_far(it, 0, 1)
        rise(it, 1, 2)
        primal(it, 1, 0)
        forward_near(it, 0, 0)
        rise(it, 1, 3)
        forward_near(it, 0, 1)
        primal(it, 1, 1)
        primal(it, 1, 2)
        primal(it, 1, 3)
        forward_far(it, 1, 0)
        y_sum(it, 0, 0)
        forward_far(it, 1, 1)
        y_sum(it, 0, 1)
        forward_near(it, 1, 0)
        forward_near(it, 1, 1)
        dual(it, 0)
        last = it == ITERS - 1
        if not last:
            price_rows(it + 1, 0, 0, block_rows)
        y_sum(it, 1, 0)
        y_sum(it, 1, 1)
        if not last:
            scatter(it + 1, 0)
        dual(it, 1)
        if not last:
            price_rows(it + 1, 1, 0, block_rows)
    for h in range(GROUPS):
        next_weight(ITERS - 1, h)
        weight_out[scen_rows(h), :] = jnp.broadcast_to(weights[h], (span, 128))

    for c in pending:
        c.wait_send()
    for b in range(ITERS * GROUPS):
        for g in range(CHUNKS):
            z_line.drain(b, g)
        for g in range(Y_CHUNKS):
            y_line.drain(b, g)


def finish(rates, duals, weight, rates_out, duals_out, weight_out):
    rates_out[...] = rates[...]
    duals_out[...] = duals[...]
    scen = weight_out.shape[0]
    shape = weight.shape
    here = lax.broadcasted_iota(jnp.int32, shape, 0) == lax.broadcasted_iota(jnp.int32, shape, 1)
    weight_out[...] = jnp.sum(jnp.where(here, weight[...], 0.0), axis=0)[:scen]


def body(tiles, tile_index, tiles_in_use, demand, profiles, capacity, start_rates, start_duals, primal_weight):
    rows_n = lax.axis_size("rows")
    blk_n = lax.axis_size("blk")
    block_rows, _, slots, tile, _ = tiles.shape
    scen, width = profiles.shape
    dual_width = capacity.shape[1]
    blocks = width // tile
    span = scen // GROUPS
    nb = ITERS * GROUPS
    half = block_rows // 2
    vmem = pl.BlockSpec(memory_space=pltpu.VMEM)
    smem = pl.BlockSpec(memory_space=pltpu.SMEM)
    hbm = pl.BlockSpec(memory_space=pl.ANY)
    dma = pltpu.SemaphoreType.DMA
    w_buf = pltpu.VMEM((block_rows * slots, tile, tile), BF16)
    z_buf = pltpu.VMEM((nb, blocks, span, tile), F32)
    y_buf = pltpu.VMEM((nb, half, span, tile), F32)
    rates, duals, weight = pl.pallas_call(
        functools.partial(kernel, rows_n, blk_n),
        out_shape=(
            jax.ShapeDtypeStruct((scen, width), F32),
            jax.ShapeDtypeStruct((scen, dual_width), F32),
            jax.ShapeDtypeStruct((scen, 128), F32),
        ),
        in_specs=[hbm, hbm, hbm, smem, vmem, vmem, vmem, vmem, smem],
        out_specs=(vmem, vmem, vmem),
        scratch_shapes=[
            pltpu.VMEM((block_rows, slots, tile, tile), F32),
            w_buf, w_buf, w_buf, w_buf,
            pltpu.VMEM((scen, width), F32),
            pltpu.VMEM((scen, 128), F32),
            pltpu.SMEM((slots, block_rows), jnp.int32),
            pltpu.SMEM((1, block_rows), jnp.int32),
            pltpu.VMEM((GROUPS, blocks, 2 * span, tile), BF16),
            pltpu.VMEM((block_rows * slots, span, tile), F32),
            z_buf, z_buf, z_buf,
            y_buf, y_buf, y_buf, y_buf, y_buf, y_buf,
            pltpu.VMEM((nb, blk_n, span, 128), F32),
            pltpu.VMEM((nb, rows_n, span, 128), F32),
            dma((block_rows,)), dma((2,)),
            dma((nb * CHUNKS,)), dma((nb * CHUNKS,)), dma((nb * CHUNKS,)), dma((nb * CHUNKS,)),
            dma((nb * Y_CHUNKS,)), dma((nb * Y_CHUNKS,)), dma((nb * Y_CHUNKS,)), dma((nb * Y_CHUNKS,)),
            dma((nb * Y_CHUNKS,)), dma((nb * Y_CHUNKS,)), dma((nb * Y_CHUNKS,)), dma((nb * Y_CHUNKS,)),
            dma((nb * blk_n,)), dma((nb * blk_n,)), dma((nb * rows_n,)), dma((nb * rows_n,)),
        ],
        compiler_params=pltpu.CompilerParams(
            collective_id=0, has_side_effects=True, vmem_limit_bytes=60 * 1024 * 1024
        ),
    )(
        tiles, tile_index[:, 0].T, tiles_in_use.T, demand, profiles, capacity, start_rates, start_duals,
        primal_weight,
    )
    return pl.pallas_call(
        finish,
        out_shape=(
            jax.ShapeDtypeStruct(rates.shape, F32),
            jax.ShapeDtypeStruct(duals.shape, F32),
            jax.ShapeDtypeStruct((scen,), F32),
        ),
        in_specs=[vmem, vmem, vmem],
        out_specs=(vmem, vmem, vmem),
    )(rates, duals, weight)


def solution(mesh):
    placed = (
        P(("groups", "rows"), "blk", None, None, None),
        P(("groups", "rows"), "blk", None),
        P(("groups", "rows"), "blk"),
        P("groups"),
        P("groups", "blk"),
        P("groups", "rows"),
        P("groups", "blk"),
        P("groups", "rows"),
        P("groups"),
    )
    return jax.shard_map(
        body,
        mesh=mesh,
        in_specs=placed,
        out_specs=(P("groups", "blk"), P("groups", "rows"), P("groups")),
        check_vma=False,
    )
```
